512 devices in a mesh: gx: 64 (over y, x, z_hi, core), gy: 8 (over z_lo).
Axes of the slice: x: 4, y: 4, z: 16 (z_hi: 2, z_lo: 8; z = z_hi * 8 + z_lo), core: 2. Of those that a mesh axis runs over, the one named last changes fastest.
Arguments:
- adjoint_init: float32 [3, 512, 64, 256], P(None, 'gx', 'gy'), may hold values from -6 to 6
- saved_states: bfloat16 [4, 3, 512, 64, 256], P(None, None, 'gx', 'gy'), may hold values from -4 to 4
- step_index: int32 [4], replicated, may hold values from 0 to 3
- vertical_inverse: float32 [256, 256], replicated, may hold values from -1 to 2
- disk_filter: bfloat16 [64, 8, 8, 64, 512], P('gx', 'gy'), may hold values from -0.25 to 0.25
- pair_turbine: int32 [64, 8, 8], P('gx', 'gy'), may hold values from 0 to 96, as said below
- pair_tile: int32 [64, 8, 8], P('gx', 'gy'), may hold values from 0 to 31
- turbine_owner: int32 [96], replicated, may hold values from 0 to 511
Outputs:
- adjoint_final: float32 [3, 512, 64, 256], P(None, 'gx', 'gy')
- turbine_grad: float32 [64, 8, 96], P('gx', 'gy')
The draws below stay inside these ranges and needn't reach their ends.
Inputs may be any that keep to these rules, and one draw needn't show every extreme that they name: `pair_turbine`: entry 96 marks an empty slot.
All inputs are finite; a program needn't handle non-finite values.
Results may differ from the reference program's by a relative error of at most 0.0024.
Values may be sent and summed in bfloat16 or wider, within the bound.
No kernel may reach another device: no remote copies, remote signals or barrier semaphores. Data moves between devices by JAX's collectives and lax.ppermute only.
A program may use at most 64 MiB of HBM per device.

```python
import math
import jax
import jax.numpy as jnp
from jax import lax

CX = 8
CY = 8
NZ = 256
DISK = 64
STEPS = 4
SAVED = 4
SLOTS = 8
TURB_SLAB = 12
TILE = 512
TURB = 96
NDEV = 512
NX = 512
NY = 64
N_GX = 64
N_GY = 8


def draw_vertical_inverse(key, part):
    first_key, second_key = jax.random.split(jax.random.fold_in(key, 11))
    diagonal = jax.random.uniform(first_key, (NZ,), jnp.float32, 0.6, 1.0)
    noise = jax.random.normal(second_key, (NZ, NZ), jnp.float32) / (2.5 * math.sqrt(NZ))
    noise = jnp.clip(noise, -6.0 / (2.5 * math.sqrt(NZ)), 6.0 / (2.5 * math.sqrt(NZ)))
    return (noise + jnp.diag(diagonal)).astype(jnp.float32)


def slab_layout(slab_key):
    first_key, second_key, third_key = jax.random.split(slab_key, 3)
    scores = jax.random.permutation(first_key, N_GX).astype(jnp.int32)
    leading = jax.random.randint(second_key, (), 0, N_GX).astype(jnp.int32)
    follower = (leading + 1) % N_GX
    places = jnp.arange(N_GX, dtype=jnp.int32)
    scores = jnp.where(places == leading, -2, jnp.where(places == follower, -1, scores))
    positions = jnp.argsort(scores, stable=True)[:TURB_SLAB].astype(jnp.int32)
    holder = jnp.full((N_GX,), TURB_SLAB, jnp.int32).at[positions].set(jnp.arange(TURB_SLAB, dtype=jnp.int32))
    spans = jax.random.randint(third_key, (TURB_SLAB,), 0, CY // 2 - 1).astype(jnp.int32)
    spans = spans.at[0].set(CY // 2 - 2)
    return (holder, spans)


def layout_tables(key):
    base = jax.random.fold_in(key, 5)
    slab_keys = jax.random.split(base, N_GY)
    holders, spans = jax.vmap(slab_layout)(slab_keys)
    spans = jnp.concatenate([spans, jnp.zeros((N_GY, 1), jnp.int32)], axis=1)
    left = jnp.transpose(holders)
    right = jnp.roll(left, 1, axis=0)
    slab_ids = jnp.arange(N_GY, dtype=jnp.int32)[None, :]
    half_span = CY // 2
    offsets_x = jnp.array([0, 0, 1, 1], jnp.int32)
    offsets_y = jnp.array([0, 1, 0, 1], jnp.int32)
    left_span = spans[slab_ids, left]
    right_span = spans[slab_ids, right]
    left_tiles = (CX - 2 + offsets_x)[None, None, :] * half_span + left_span[:, :, None] + offsets_y[None, None, :]
    right_tiles = offsets_x[None, None, :] * half_span + right_span[:, :, None] + offsets_y[None, None, :]
    left_live = (left < TURB_SLAB)[:, :, None]
    right_live = (right < TURB_SLAB)[:, :, None]
    left_ids = jnp.where(left_live, slab_ids[:, :, None] * TURB_SLAB + left[:, :, None], TURB) * jnp.ones((1, 1, 4), jnp.int32)
    right_ids = jnp.where(right_live, slab_ids[:, :, None] * TURB_SLAB + right[:, :, None], TURB) * jnp.ones((1, 1, 4), jnp.int32)
    left_tiles = jnp.where(left_live, left_tiles, 0)
    right_tiles = jnp.where(right_live, right_tiles, 0)
    turbine_ids = jnp.concatenate([left_ids, right_ids], axis=2).astype(jnp.int32)
    tile_ids = jnp.concatenate([left_tiles, right_tiles], axis=2).astype(jnp.int32)
    return (turbine_ids, tile_ids)


def draw_pair_turbine(key, part):
    return layout_tables(key)[0]


def draw_pair_tile(key, part):
    return layout_tables(key)[1]


def touch_ends(entries, own_key, least, high):
    place = [jax.random.randint(jax.random.fold_in(own_key, axis), (), 0, length) for axis, length in enumerate(entries.shape)]
    longest = entries.shape.index(max(entries.shape))
    beside = place[:longest] + [(place[longest] + 1) % entries.shape[longest]] + place[longest + 1:]
    return entries.at[tuple(place)].set(least).at[tuple(beside)].set(high)


def level_of(key, extent, shards, low, largest):
    level, own = 1.0, jax.random.fold_in(key, 6)
    for position, shards_of in shards:
        steps = jnp.exp(jax.random.uniform(jax.random.fold_in(own, position), (shards_of,), jnp.float32, low / len(shards), largest / len(shards)))
        level = level * jnp.repeat(steps, extent[position] // shards_of).reshape([-1 if axis == position else 1 for axis in range(len(extent))])
    return level


def scatter_about(rng, shape, scale, most, pieces=(), kind=jnp.bfloat16):
    factor_of = level_of(rng, shape, pieces, -0.22, 0.18) if pieces else 1.0
    entries = jax.random.normal(rng, shape, jnp.float32) * scale * factor_of
    return jnp.minimum(jnp.maximum(entries, -most), most).astype(kind)


def setup_inputs(seed: int = 0) -> dict:
    key_list = jax.random.split(jax.random.key(seed), 9)
    adjoint_init = scatter_about(key_list[0], (3, NX, NY, NZ), 1.0, 6.0, ((1, 64), (2, 8)), jnp.float32)
    saved_states = scatter_about(key_list[1], (SAVED, 3, NX, NY, NZ), 0.7, 4.0, ((2, 64), (3, 8)))
    step_index = touch_ends(jax.random.randint(key_list[2], (STEPS,), 0, SAVED), jax.random.fold_in(key_list[2], 1), 0, SAVED - 1).astype(jnp.int32)
    vertical_inverse = draw_vertical_inverse(jax.random.fold_in(key_list[8], 71), 0)
    disk_filter = scatter_about(key_list[4], (N_GX, N_GY, SLOTS, DISK, TILE), TILE ** -0.5, 0.25, ((0, 64), (1, 8)))
    pair_turbine = draw_pair_turbine(jax.random.fold_in(key_list[8], 71), 0)
    pair_tile = draw_pair_tile(jax.random.fold_in(key_list[8], 71), 0)
    turbine_owner = touch_ends(jax.random.randint(key_list[7], (TURB,), 0, NDEV), jax.random.fold_in(key_list[7], 1), 0, NDEV - 1).astype(jnp.int32)
    return {"adjoint_init": adjoint_init, "saved_states": saved_states, "step_index": step_index, "vertical_inverse": vertical_inverse, "disk_filter": disk_filter, "pair_turbine": pair_turbine, "pair_tile": pair_tile, "turbine_owner": turbine_owner}


COURANT = 0.2


def periodic_difference(values, axis):
    return 0.5 * (jnp.roll(values, -1, axis) - jnp.roll(values, 1, axis))


def vertical_difference(values):
    padded = jnp.pad(values, ((0, 0), (0, 0), (1, 1)))
    return 0.5 * (padded[:, :, 2:] - padded[:, :, :-2])


def reference(adjoint_init, saved_states, step_index, vertical_inverse, disk_filter, pair_turbine, pair_tile, turbine_owner):
    adjoint = adjoint_init
    gradient = jnp.zeros((TURB,), jnp.float32)
    filters = disk_filter.astype(jnp.float32)
    half_span = CY // 2
    stream_index = jnp.arange(N_GX, dtype=jnp.int32)[:, None, None] * CX + pair_tile // half_span
    span_index = jnp.arange(N_GY, dtype=jnp.int32)[None, :, None] * half_span + pair_tile % half_span
    onehot = (pair_turbine[..., None] == jnp.arange(TURB, dtype=jnp.int32)).astype(jnp.float32)
    for number in range(STEPS):
        stored = lax.dynamic_index_in_dim(saved_states, step_index[number].astype(jnp.int32), 0, keepdims=False)
        forward = stored.astype(jnp.float32)
        derivs = [[periodic_difference(forward[source], 0), periodic_difference(forward[source], 1), vertical_difference(forward[source])] for source in range(3)]
        solved = jnp.dot(adjoint.reshape(-1, NZ), vertical_inverse, precision=lax.Precision.HIGHEST, preferred_element_type=jnp.float32).reshape(adjoint.shape)
        updated = []
        for component in range(3):
            current = solved[component]
            advect = forward[0] * periodic_difference(current, 0) + forward[1] * periodic_difference(current, 1) + forward[2] * vertical_difference(current)
            couple = solved[0] * derivs[0][component] + solved[1] * derivs[1][component] + solved[2] * derivs[2][component]
            updated.append(current + COURANT * (advect - couple))
        adjoint = jnp.stack(updated)
        adjoint_tiles = adjoint[0].astype(jnp.bfloat16).reshape(NX, NY // 2, 2 * NZ)
        speed_tiles = stored[0].reshape(NX, NY // 2, 2 * NZ)
        picked_adjoint = adjoint_tiles[stream_index, span_index].astype(jnp.float32)
        picked_speed = speed_tiles[stream_index, span_index].astype(jnp.float32)
        sampled = jnp.einsum("ikjpt,ikjt->ikjp", filters, picked_adjoint, precision=lax.Precision.HIGHEST)
        speeds = jnp.einsum("ikjpt,ikjt->ikjp", filters, picked_speed, precision=lax.Precision.HIGHEST)
        contribs = jnp.mean(speeds * speeds * sampled, axis=-1)
        gradient = gradient + jnp.sum(contribs[..., None] * onehot, axis=(0, 1, 2))
    device_ids = jnp.arange(N_GX, dtype=jnp.int32)[:, None] * N_GY + jnp.arange(N_GY, dtype=jnp.int32)[None, :]
    owned_mask = turbine_owner[None, None, :] == device_ids[:, :, None]
    turbine_grad = jnp.where(owned_mask, gradient[None, None, :], jnp.float32(0.0))
    return adjoint, turbine_grad
```

```python
import functools

import jax
import jax.numpy as jnp
from jax import lax
from jax.experimental import pallas as pl
from jax.experimental.pallas import tpu as pltpu
from jax.sharding import Mesh
from jax.sharding import PartitionSpec as P

STEPS = 4
GX = ("gx_0", "gx_1", "gx_2", "gx_3")
NEAR_AXES = ("gx_0", "gx_1", "gx_3")
FAR_AXES = ("gx_2", "gy")
TENTH = 0.2 * 0.5
RADII = (4, 4, 3, 2, 1, 2)
REST = 5
LEVELS = 256


def x_base(field):
    return 3 * sum(RADII[:field])


def x_tile(field, c, d):
    return x_base(field) + c * RADII[field] + d - 1


X_TILES = x_base(len(RADII))


def y_pairs(field):
    return 3 + RADII[field]


def y_tile(field, c, i):
    return 3 * sum(y_pairs(f) for f in range(field)) + c * y_pairs(field) + i


Y_TILES = y_tile(len(RADII) - 1, 2, y_pairs(len(RADII) - 1) - 1) + 1


def own_column(adj_ref, st_ref, place, field, c, x):
    if field == 0:
        return adj_ref[c, x]
    if field == REST:
        return adj_ref[c, x] - adj_ref[c, x].astype(jnp.bfloat16).astype(jnp.float32)
    return st_ref[place[field - 1], c, x]


def pack_x(place, adj_ref, st_ref, far_ref, near_ref):
    first = place[4] == 0
    for field, radius in enumerate(RADII):
        for d in range(1, radius + 1):
            far_x = jnp.where(first, d - 1, 8 - d)
            near_x = jnp.where(first, 8 - d, d - 1)
            for c in range(3):
                n = x_tile(field, c, d)
                far_ref[n] = own_column(adj_ref, st_ref, place, field, c, far_x).astype(jnp.bfloat16)
                near_ref[n] = own_column(adj_ref, st_ref, place, field, c, near_x).astype(jnp.bfloat16)


def column(place, adj_ref, st_ref, far_ref, near_ref, field, c, x):
    if 0 <= x < 8:
        return own_column(adj_ref, st_ref, place, field, c, x).astype(jnp.float32)
    n = x_tile(field, c, -x if x < 0 else x - 7)
    far, near = far_ref[n].astype(jnp.float32), near_ref[n].astype(jnp.float32)
    return jnp.where((place[4] == 0) == (x < 0), far, near)


def low_half():
    return lax.broadcasted_iota(jnp.int32, (8, LEVELS), 0) < 4


def swap_halves(tile):
    return pltpu.roll(tile, 4, 0)


def pack_y(place, adj_ref, st_ref, far_ref, near_ref, even_ref, odd_ref):
    even = place[5] == 0
    low = low_half()
    for field, radius in enumerate(RADII):
        for c in range(3):
            for i in range(y_pairs(field)):
                x = 2 * i - (radius - 1)
                left = column(place, adj_ref, st_ref, far_ref, near_ref, field, c, x)
                right = column(place, adj_ref, st_ref, far_ref, near_ref, field, c, x + 1)
                bottom = jnp.where(low, left, swap_halves(right))
                top = jnp.where(low, swap_halves(left), right)
                n = y_tile(field, c, i)
                even_ref[n] = jnp.where(even, top, bottom).astype(jnp.bfloat16)
                odd_ref[n] = jnp.where(even, bottom, top).astype(jnp.bfloat16)


def sweep(
    place,
    tiles,
    turbines,
    adj_ref,
    st_ref,
    far_ref,
    near_ref,
    even_ref,
    odd_ref,
    whi_ref,
    wlo_ref,
    dz_ref,
    filt_ref,
    out_ref,
    part_ref,
    ext,
    solved,
    state_dz,
    kept,
    picked,
):
    even = place[5] == 0
    low = low_half()
    for field, radius in enumerate(RADII):
        into = 0 if field == REST else field
        for c in range(3):
            for x in range(-radius, 8 + radius):
                if field == REST and 0 <= x < 8:
                    continue
                tile = column(place, adj_ref, st_ref, far_ref, near_ref, field, c, x)
                if field == REST:
                    tile += ext[0, c, x + 4, 0:8, :]
                ext[into, c, x + 4, 0:8, :] = tile
            for i in range(y_pairs(field)):
                x = 2 * i - (radius - 1)
                n = y_tile(field, c, i)
                a, b = even_ref[n].astype(jnp.float32), odd_ref[n].astype(jnp.float32)
                plus, minus = jnp.where(even, a, b), jnp.where(even, b, a)
                left = jnp.where(low, plus, swap_halves(minus))
                right = jnp.where(low, swap_halves(plus), minus)
                if field == REST:
                    left += ext[0, c, x + 4, 8:16, :]
                    right += ext[0, c, x + 5, 8:16, :]
                ext[into, c, x + 4, 8:16, :] = left
                ext[into, c, x + 5, 8:16, :] = right

    for step in range(STEPS):
        reach = 3 - step
        lo, hi = 4 - reach, 12 + reach
        wide = hi - lo + 2
        rows = ext[0, :, lo - 1 : hi + 1].reshape(3 * wide * 16, LEVELS)
        upper = rows.astype(jnp.bfloat16)
        lower = (rows - upper.astype(jnp.float32)).astype(jnp.bfloat16)
        for half in range(2):
            lanes = slice(half * LEVELS, (half + 1) * LEVELS)
            total = jnp.dot(upper, whi_ref[:, lanes], preferred_element_type=jnp.float32)
            total += jnp.dot(lower, whi_ref[:, lanes], preferred_element_type=jnp.float32)
            total += jnp.dot(upper, wlo_ref[:, lanes], preferred_element_type=jnp.float32)
            solved[half, :, lo - 1 : hi + 1] = total.reshape(3, wide, 16, LEVELS)
        field = 1 + step
        states = ext[field, :, lo:hi].reshape(3 * (wide - 2) * 16, LEVELS).astype(jnp.bfloat16)
        state_dz[:, lo:hi] = jnp.dot(
            states, dz_ref[...], preferred_element_type=jnp.float32
        ).reshape(3, wide - 2, 16, LEVELS)

        def one(e, carry):
            def across(ref, *at):
                return ref[(*at, e + 1)] - ref[(*at, e - 1)]

            def along(tile):
                return pltpu.roll(tile, 15, 0) - pltpu.roll(tile, 1, 0)

            sol = [solved[0, c, e] for c in range(3)]
            vel = [ext[field, c, e] for c in range(3)]
            derivs = (
                [across(ext, field, c) for c in range(3)],
                [along(vel[c]) for c in range(3)],
                [state_dz[c, e] for c in range(3)],
            )
            for c in range(3):
                advect = vel[0] * across(solved, 0, c) + vel[1] * along(sol[c]) + vel[2] * solved[1, c, e]
                couple = sol[0] * derivs[c][0] + sol[1] * derivs[c][1] + sol[2] * derivs[c][2]
                ext[0, c, e] = sol[c] + TENTH * (advect - couple)
            return carry

        lax.fori_loop(lo, hi, one, 0)
        kept[step] = ext[0, 0, 4:12, 0:8, :]

    out_ref[...] = ext[0, :, 4:12, 0:8, :]
    lane = lax.broadcasted_iota(jnp.int32, (1, 128), 1)
    total = jnp.zeros((1, 128), jnp.float32)
    for slot in range(8):
        tile = tiles[slot]
        x, y = tile // 4, 2 * lax.rem(tile, 4)
        for step in range(STEPS):
            for k in range(2):
                lanes = slice(k * LEVELS, (k + 1) * LEVELS)
                picked[slot, step : step + 1, lanes] = kept[step, x, pl.ds(y + k, 1), :]
                picked[slot, 4 + step : 5 + step, lanes] = ext[1 + step, 0, x + 4, pl.ds(y + k, 1), :]
        both = lax.dot_general(
            picked[slot].astype(jnp.bfloat16),
            filt_ref[slot],
            (((1,), (1,)), ((), ())),
            preferred_element_type=jnp.float32,
        )
        sampled, speeds = both[0:4], both[4:8]
        term = jnp.sum(jnp.sum(speeds * speeds * sampled, axis=1, keepdims=True), axis=0, keepdims=True)
        total += jnp.where(lane == turbines[slot], term * (1.0 / 64.0), 0.0)
    part_ref[...] = jnp.broadcast_to(total, part_ref.shape)


SMEM = pl.BlockSpec(memory_space=pltpu.SMEM)
VMEM = pl.BlockSpec(memory_space=pltpu.VMEM)


def body(
    adjoint_init,
    saved_states,
    step_index,
    vertical_inverse,
    disk_filter,
    pair_turbine,
    pair_tile,
    turbine_owner,
):
    turbines = turbine_owner.shape[0]
    place = jnp.concatenate(
        [
            step_index.astype(jnp.int32),
            lax.axis_index("gx_3").astype(jnp.int32)[None],
            lax.rem(lax.axis_index("gy"), 2).astype(jnp.int32)[None],
        ]
    )
    blocks, slabs = lax.axis_size(GX), lax.axis_size("gy")
    near = [(i, i ^ 1) for i in range(blocks)]
    far = [(i, (i + 1) % blocks if i % 2 else (i - 1) % blocks) for i in range(blocks)]
    evens = [(i, i ^ 1) for i in range(slabs)]
    odds = [(i, (i + 1) % slabs if i % 2 else (i - 1) % slabs) for i in range(slabs)]

    x_shape = jax.ShapeDtypeStruct((X_TILES, 8, LEVELS), jnp.bfloat16)
    y_shape = jax.ShapeDtypeStruct((Y_TILES, 8, LEVELS), jnp.bfloat16)
    to_far, to_near = pl.pallas_call(
        pack_x,
        out_shape=(x_shape, x_shape),
        in_specs=[SMEM, VMEM, VMEM],
        out_specs=(VMEM, VMEM),
        name="pack_x",
    )(place, adjoint_init, saved_states)
    far_halo = lax.ppermute(to_far, GX, far)
    near_halo = lax.ppermute(to_near, GX, near)

    inverse_dz = jnp.pad(vertical_inverse[:, 1:], ((0, 0), (0, 1))) - jnp.pad(
        vertical_inverse[:, :-1], ((0, 0), (1, 0))
    )
    weights = jnp.concatenate([vertical_inverse, inverse_dz], axis=1)
    upper = lax.reduce_precision(weights, 8, 7)
    whi, wlo = upper.astype(jnp.bfloat16), (weights - upper).astype(jnp.bfloat16)
    k = lax.broadcasted_iota(jnp.int32, (LEVELS, LEVELS), 0)
    z = lax.broadcasted_iota(jnp.int32, (LEVELS, LEVELS), 1)
    dz = ((k == z + 1).astype(jnp.float32) - (k == z - 1).astype(jnp.float32)).astype(jnp.bfloat16)

    to_even, to_odd = pl.pallas_call(
        pack_y,
        out_shape=(y_shape, y_shape),
        in_specs=[SMEM] + [VMEM] * 4,
        out_specs=(VMEM, VMEM),
        name="pack_y",
    )(place, adjoint_init, saved_states, far_halo, near_halo)
    odd_halo = lax.ppermute(to_odd, "gy", odds)
    even_halo = lax.ppermute(to_even, "gy", evens)

    close = lax.axis_size(NEAR_AXES)
    wide = lax.axis_size(FAR_AXES)
    adjoint, part = pl.pallas_call(
        sweep,
        out_shape=(
            jax.ShapeDtypeStruct(adjoint_init.shape, jnp.float32),
            jax.ShapeDtypeStruct((close, 128), jnp.float32),
        ),
        in_specs=[SMEM] * 3 + [VMEM] * 10,
        out_specs=(VMEM, VMEM),
        scratch_shapes=[
            pltpu.VMEM((5, 3, 16, 16, LEVELS), jnp.float32),
            pltpu.VMEM((2, 3, 16, 16, LEVELS), jnp.float32),
            pltpu.VMEM((3, 16, 16, LEVELS), jnp.float32),
            pltpu.VMEM((STEPS, 8, 8, LEVELS), jnp.float32),
            pltpu.VMEM((8, 8, 2 * LEVELS), jnp.float32),
        ],
        name="sweep",
    )(
        place,
        pair_tile[0, 0],
        pair_turbine[0, 0],
        adjoint_init,
        saved_states,
        far_halo,
        near_halo,
        even_halo,
        odd_halo,
        whi,
        wlo,
        dz,
        disk_filter[0, 0],
    )
    part = jnp.sum(lax.all_to_all(part, NEAR_AXES, 0, 0, tiled=True), axis=0)
    part = jnp.broadcast_to(part[None], (wide, 128))
    totals = jnp.sum(lax.all_to_all(part, FAR_AXES, 0, 0, tiled=True), axis=0)[:turbines]
    own_index = lax.axis_index(GX) * lax.axis_size("gy") + lax.axis_index("gy")
    turbine_grad = jnp.where(turbine_owner == own_index, totals, jnp.float32(0.0))[None, None, :]
    return (adjoint, turbine_grad)


def solution(mesh):
    torus = Mesh(
        mesh.devices.reshape(4, 4, 2, 2, mesh.shape["gy"]), ("gx_0", "gx_1", "gx_2", "gx_3", "gy")
    )
    placed = (
        P(None, GX, "gy", None),
        P(None, None, GX, "gy", None),
        P(),
        P(),
        P(GX, "gy", None, None, None),
        P(GX, "gy", None),
        P(GX, "gy", None),
        P(),
    )
    return jax.shard_map(
        body,
        mesh=torus,
        in_specs=placed,
        out_specs=(P(None, GX, "gy", None), P(GX, "gy", None)),
        check_vma=False,
    )
```

```python
import jax
import jax.numpy as jnp
from jax import lax
from jax.experimental import pallas as pl
from jax.experimental.pallas import tpu as pltpu
from jax.sharding import Mesh
from jax.sharding import PartitionSpec as P

STEPS = 4
GX = ("gx_0", "gx_1", "gx_2", "gx_3")
NEAR_AXES = ("gx_0", "gx_1", "gx_3")
FAR_AXES = ("gx_2", "gy")
TENTH = 0.2 * 0.5
LEVELS = 256
RADII = (4, 4, 3, 2, 1, 2)
REST = 5


def padded(rows):
    return (rows + 15) // 16 * 16


def enumerate_runs(lengths):
    offsets, at = {}, 0
    for key, length in lengths:
        offsets[key] = at
        at += length
    return offsets, padded(at)


EDGE_RUNS, EDGE_ROWS = enumerate_runs(
    ((f, c, d, k), r - d) for f, r in enumerate(RADII) for c in range(3) for d in range(1, r) for k in range(2)
)
CORE_RUNS, CORE_ROWS = enumerate_runs(
    ((f, c, d), 8 - 2 * (r - d)) for f, r in enumerate(RADII) for c in range(3) for d in range(1, r + 1)
)
NEAR_RUNS, NEAR_ROWS = enumerate_runs(
    ((f, c, d), 8) for f, r in enumerate(RADII) for c in range(3) for d in range(1, r + 1)
)
Y_RUNS, Y_ROWS = enumerate_runs(
    [((f, c, d), 8) for f, r in enumerate(RADII) for c in range(3) for d in range(1, r + 1)]
    + [((f, c, d, k), r - d) for f, r in enumerate(RADII) for c in range(3) for d in range(1, r) for k in range(2)]
)


def first_core():
    return lax.axis_index("gx_3") == 0


def even_slab():
    return lax.rem(lax.axis_index("gy"), 2) == 0


def own_column(steps, adj_ref, st_ref, first, field, c, p):
    x = jnp.where(first, p, 7 - p)
    if field == 0:
        return adj_ref[c, x]
    if field == REST:
        tile = adj_ref[c, x]
        return tile - tile.astype(jnp.bfloat16).astype(jnp.float32)
    return st_ref[steps[field - 1], c, x].astype(jnp.float32)


def pack_x(steps, adj_ref, st_ref, edge_ref, core_ref, near_ref, edge, core):
    first = first_core()
    for field, radius in enumerate(RADII):
        for c in range(3):
            for d in range(1, radius + 1):
                tile = own_column(steps, adj_ref, st_ref, first, field, c, d - 1)
                length = radius - d
                if length:
                    at = EDGE_RUNS[field, c, d, 0]
                    edge[at : at + length, :] = tile[:length]
                    at = EDGE_RUNS[field, c, d, 1]
                    edge[at : at + length, :] = tile[8 - length :]
                at = CORE_RUNS[field, c, d]
                core[at : at + 8 - 2 * length, :] = tile[length : 8 - length]
                at = NEAR_RUNS[field, c, d]
                near_ref[at : at + 8, :] = own_column(
                    steps, adj_ref, st_ref, first, field, c, 8 - d
                ).astype(jnp.bfloat16)
    edge_ref[...] = edge[...].astype(jnp.bfloat16)
    core_ref[...] = core[...].astype(jnp.bfloat16)


def pack_y(steps, adj_ref, st_ref, edge_ref, near_ref, odd_ref, even_ref, wide, edge, flat):
    first, even = first_core(), even_slab()
    edge[...] = edge_ref[...].astype(jnp.float32)

    def put(field, c, at, rows):
        wide[field, c, 0, at, :] = rows[:, :128]
        wide[field, c, 1, at, :] = rows[:, 128:]

    for field, radius in enumerate(RADII):
        for c in range(3):
            for p in range(8):
                at = (p + 4) * 8
                put(field, c, slice(at, at + 8), own_column(steps, adj_ref, st_ref, first, field, c, p))
            for d in range(1, radius):
                length = radius - d
                at = (4 - d) * 8
                run = EDGE_RUNS[field, c, d, 0]
                put(field, c, slice(at, at + length), edge[run : run + length, :])
                run = EDGE_RUNS[field, c, d, 1]
                put(field, c, slice(at + 8 - length, at + 8), edge[run : run + length, :])
                at, run = (11 + d) * 8, NEAR_RUNS[field, c, d]
                put(field, c, slice(at, at + 8), near_ref[run : run + 8, :].astype(jnp.float32))

    def take(field, c, run, start, length):
        at = pl.ds(start, length, stride=8)
        flat[run : run + length, 0:128] = wide[field, c, 0, at, :]
        flat[run : run + length, 128:256] = wide[field, c, 1, at, :]

    for side, out in enumerate((odd_ref, even_ref)):
        up = even if side else jnp.logical_not(even)
        for field, radius in enumerate(RADII):
            for c in range(3):
                for d in range(1, radius + 1):
                    y = jnp.where(up, 8 - d, d - 1)
                    length = radius - d
                    take(field, c, Y_RUNS[field, c, d], 4 * 8 + y, 8)
                    if length:
                        take(field, c, Y_RUNS[field, c, d, 0], (4 - length) * 8 + y, length)
                        take(field, c, Y_RUNS[field, c, d, 1], 12 * 8 + y, length)
        out[...] = flat[...].astype(jnp.bfloat16)


def rest_reach(e):
    p = e - 4
    return max(0, RADII[REST] - max(0, -p, p - 7))


def sweep(
    steps,
    tiles,
    turbines,
    adj_ref,
    st_ref,
    edge_ref,
    core_ref,
    near_ref,
    odd_ref,
    even_ref,
    whi_ref,
    wlo_ref,
    dz_ref,
    filt_ref,
    out_ref,
    part_ref,
    ext,
    solved,
    state_dz,
    kept,
    picked,
    edge,
    core,
    flat,
    wide,
):
    first, even = first_core(), even_slab()
    sign = jnp.where(first, 1.0, -1.0).astype(jnp.float32)
    edge[...] = edge_ref[...].astype(jnp.float32)
    core[...] = core_ref[...].astype(jnp.float32)
    for field, radius in enumerate(RADII):
        into = 0 if field == REST else field

        def put(c, at, rows):
            old = ext[0, c, at, :] if field == REST else 0.0
            ext[into, c, at, :] = rows + old

        for c in range(3):
            if field != REST:
                for p in range(8):
                    put(c, slice((p + 4) * 16, (p + 4) * 16 + 8), own_column(steps, adj_ref, st_ref, first, field, c, p))
            for d in range(1, radius + 1):
                at, length = (4 - d) * 16, radius - d
                if length:
                    for k, y in ((0, 0), (1, 8 - length)):
                        run = EDGE_RUNS[field, c, d, k]
                        put(c, slice(at + y, at + y + length), edge[run : run + length, :])
                run = CORE_RUNS[field, c, d]
                put(c, slice(at + length, at + 8 - length), core[run : run + 8 - 2 * length, :])
                at, run = (11 + d) * 16, NEAR_RUNS[field, c, d]
                put(c, slice(at, at + 8), near_ref[run : run + 8, :].astype(jnp.float32))

    def spread(field, c, run, start, length):
        at = pl.ds(start, length, stride=8)
        wide[field, c, 0, at, :] = flat[run : run + length, 0:128]
        wide[field, c, 1, at, :] = flat[run : run + length, 128:256]

    for side, halo in enumerate((odd_ref, even_ref)):
        up = even if side else jnp.logical_not(even)
        flat[...] = halo[...].astype(jnp.float32)
        for field, radius in enumerate(RADII):
            for c in range(3):
                for d in range(1, radius + 1):
                    y = jnp.where(up, d - 1, 8 - d)
                    length = radius - d
                    spread(field, c, Y_RUNS[field, c, d], 4 * 8 + y, 8)
                    if length:
                        spread(field, c, Y_RUNS[field, c, d, 0], (4 - length) * 8 + y, length)
                        spread(field, c, Y_RUNS[field, c, d, 1], 12 * 8 + y, length)
    for field, radius in enumerate(RADII[:REST]):
        for c in range(3):
            for e in range(5 - radius, 11 + radius):
                for half in range(2):
                    rows = wide[field, c, half, e * 8 : e * 8 + 8, :]
                    if field == 0:
                        near_rows = wide[REST, c, half, e * 8 : e * 8 + 8, :]
                        y = lax.broadcasted_iota(jnp.int32, (8, 128), 0)
                        reach = rest_reach(e)
                        if reach:
                            rows += jnp.where((y < reach) | (y >= 8 - reach), near_rows, 0.0)
                    ext[field, c, e * 16 + 8 : e * 16 + 16, half * 128 : half * 128 + 128] = rows

    for step in range(STEPS):
        reach = 3 - step
        lo, hi = 4 - reach, 12 + reach
        span = hi - lo + 2
        rows = ext[0, :, (lo - 1) * 16 : (hi + 1) * 16, :].reshape(3 * span * 16, LEVELS)
        upper = rows.astype(jnp.bfloat16)
        lower = (rows - upper.astype(jnp.float32)).astype(jnp.bfloat16)
        for half in range(2):
            lanes = slice(half * LEVELS, (half + 1) * LEVELS)
            total = jnp.dot(upper, whi_ref[:, lanes], preferred_element_type=jnp.float32)
            total += jnp.dot(lower, whi_ref[:, lanes], preferred_element_type=jnp.float32)
            total += jnp.dot(upper, wlo_ref[:, lanes], preferred_element_type=jnp.float32)
            solved[half, :, (lo - 1) * 16 : (hi + 1) * 16, :] = total.reshape(3, span * 16, LEVELS)
        field = 1 + step
        states = ext[field, :, lo * 16 : hi * 16, :].reshape(3 * (span - 2) * 16, LEVELS).astype(jnp.bfloat16)
        state_dz[:, lo * 16 : hi * 16, :] = jnp.dot(
            states, dz_ref[...], preferred_element_type=jnp.float32
        ).reshape(3, (span - 2) * 16, LEVELS)

        def one(e, carry):
            def at(ref, *lead, shift=0):
                return ref[(*lead, pl.ds(pl.multiple_of((e + shift) * 16, 16), 16), slice(None))]

            def across(ref, *lead):
                return at(ref, *lead, shift=1) - at(ref, *lead, shift=-1)

            def along(tile):
                return pltpu.roll(tile, 15, 0) - pltpu.roll(tile, 1, 0)

            sol = [at(solved, 0, c) for c in range(3)]
            vel = [at(ext, field, c) for c in range(3)]
            derivs = (
                [across(ext, field, c) for c in range(3)],
                [along(vel[c]) for c in range(3)],
                [at(state_dz, c) for c in range(3)],
            )
            stream = sign * vel[0]
            for c in range(3):
                advect = stream * across(solved, 0, c) + vel[1] * along(sol[c]) + vel[2] * at(solved, 1, c)
                couple = sol[0] * derivs[c][0] + sol[1] * derivs[c][1] + sol[2] * derivs[c][2]
                if c == 0:
                    couple = sign * couple
                ext[0, c, pl.ds(pl.multiple_of(e * 16, 16), 16), :] = sol[c] + TENTH * (advect - couple)
            return carry

        lax.fori_loop(lo, hi, one, 0)
        for p in range(8):
            kept[step, p * 8 : p * 8 + 8, :] = ext[0, 0, (p + 4) * 16 : (p + 4) * 16 + 8, :]

    for c in range(3):
        for p in range(8):
            out_ref[c, jnp.where(first, p, 7 - p)] = ext[0, c, (p + 4) * 16 : (p + 4) * 16 + 8, :]
    lane = lax.broadcasted_iota(jnp.int32, (1, 128), 1)
    total = jnp.zeros((1, 128), jnp.float32)
    for slot in range(8):
        tile = tiles[slot]
        x, y = tile // 4, 2 * lax.rem(tile, 4)
        p = jnp.where(first, x, 7 - x)
        for step in range(STEPS):
            for k in range(2):
                lanes = slice(k * LEVELS, (k + 1) * LEVELS)
                picked[slot, step : step + 1, lanes] = kept[step, pl.ds(p * 8 + y + k, 1), :]
                picked[slot, 4 + step : 5 + step, lanes] = ext[1 + step, 0, pl.ds((p + 4) * 16 + y + k, 1), :]
        both = lax.dot_general(
            picked[slot].astype(jnp.bfloat16),
            filt_ref[slot],
            (((1,), (1,)), ((), ())),
            preferred_element_type=jnp.float32,
        )
        sampled, speeds = both[0:4], both[4:8]
        term = jnp.sum(jnp.sum(speeds * speeds * sampled, axis=1, keepdims=True), axis=0, keepdims=True)
        total += jnp.where(lane == turbines[slot], term * (1.0 / 64.0), 0.0)
    part_ref[...] = jnp.broadcast_to(total, part_ref.shape)


SMEM = pl.BlockSpec(memory_space=pltpu.SMEM)
VMEM = pl.BlockSpec(memory_space=pltpu.VMEM)


def halo_rows(rows):
    return jax.ShapeDtypeStruct((rows, LEVELS), jnp.bfloat16)


def body(
    adjoint_init,
    saved_states,
    step_index,
    vertical_inverse,
    disk_filter,
    pair_turbine,
    pair_tile,
    turbine_owner,
):
    turbines = turbine_owner.shape[0]
    steps = step_index.astype(jnp.int32)
    blocks, slabs = lax.axis_size(GX), lax.axis_size("gy")
    near = [(i, i ^ 1) for i in range(blocks)]
    far = [(i, (i + 1) % blocks if i % 2 else (i - 1) % blocks) for i in range(blocks)]
    evens = [(i, i ^ 1) for i in range(slabs)]
    odds = [(i, (i + 1) % slabs if i % 2 else (i - 1) % slabs) for i in range(slabs)]

    to_edge, to_core, to_near = pl.pallas_call(
        pack_x,
        out_shape=(halo_rows(EDGE_ROWS), halo_rows(CORE_ROWS), halo_rows(NEAR_ROWS)),
        in_specs=[SMEM, VMEM, VMEM],
        out_specs=(VMEM,) * 3,
        scratch_shapes=[
            pltpu.VMEM((EDGE_ROWS, LEVELS), jnp.float32),
            pltpu.VMEM((CORE_ROWS, LEVELS), jnp.float32),
        ],
        compiler_params=pltpu.CompilerParams(vmem_limit_bytes=8 << 20),
        name="pack_x",
    )(steps, adjoint_init, saved_states)
    edge_halo = lax.ppermute(to_edge, GX, far)
    near_halo = lax.ppermute(to_near, GX, near)
    core_halo = lax.ppermute(to_core, GX, far)

    inverse_dz = jnp.pad(vertical_inverse[:, 1:], ((0, 0), (0, 1))) - jnp.pad(
        vertical_inverse[:, :-1], ((0, 0), (1, 0))
    )
    weights = jnp.concatenate([vertical_inverse, inverse_dz], axis=1)
    upper = lax.reduce_precision(weights, 8, 7)
    whi, wlo = upper.astype(jnp.bfloat16), (weights - upper).astype(jnp.bfloat16)
    k = lax.broadcasted_iota(jnp.int32, (LEVELS, LEVELS), 0)
    z = lax.broadcasted_iota(jnp.int32, (LEVELS, LEVELS), 1)
    dz = ((k == z + 1).astype(jnp.float32) - (k == z - 1).astype(jnp.float32)).astype(jnp.bfloat16)
    own_index = lax.axis_index(GX) * lax.axis_size("gy") + lax.axis_index("gy")
    mine = (turbine_owner == own_index).astype(jnp.float32)
    near_halo, whi, wlo, dz, mine = lax.optimization_barrier((near_halo, whi, wlo, dz, mine))

    to_odd, to_even = pl.pallas_call(
        pack_y,
        out_shape=(halo_rows(Y_ROWS), halo_rows(Y_ROWS)),
        in_specs=[SMEM] + [VMEM] * 4,
        out_specs=(VMEM, VMEM),
        scratch_shapes=[
            pltpu.VMEM((len(RADII), 3, 2, 128, 128), jnp.float32),
            pltpu.VMEM((EDGE_ROWS, LEVELS), jnp.float32),
            pltpu.VMEM((Y_ROWS, LEVELS), jnp.float32),
        ],
        compiler_params=pltpu.CompilerParams(vmem_limit_bytes=16 << 20),
        name="pack_y",
    )(steps, adjoint_init, saved_states, edge_halo, near_halo)
    odd_halo = lax.ppermute(to_odd, "gy", odds)
    even_halo = lax.ppermute(to_even, "gy", evens)

    close = lax.axis_size(NEAR_AXES)
    wide = lax.axis_size(FAR_AXES)
    adjoint, part = pl.pallas_call(
        sweep,
        out_shape=(
            jax.ShapeDtypeStruct(adjoint_init.shape, jnp.float32),
            jax.ShapeDtypeStruct((close, 128), jnp.float32),
        ),
        in_specs=[SMEM] * 3 + [VMEM] * 11,
        out_specs=(VMEM, VMEM),
        scratch_shapes=[
            pltpu.VMEM((5, 3, 256, LEVELS), jnp.float32),
            pltpu.VMEM((2, 3, 256, LEVELS), jnp.float32),
            pltpu.VMEM((3, 256, LEVELS), jnp.float32),
            pltpu.VMEM((STEPS, 64, LEVELS), jnp.float32),
            pltpu.VMEM((8, 8, 2 * LEVELS), jnp.float32),
            pltpu.VMEM((EDGE_ROWS, LEVELS), jnp.float32),
            pltpu.VMEM((CORE_ROWS, LEVELS), jnp.float32),
            pltpu.VMEM((Y_ROWS, LEVELS), jnp.float32),
            pltpu.VMEM((len(RADII), 3, 2, 128, 128), jnp.float32),
        ],
        compiler_params=pltpu.CompilerParams(vmem_limit_bytes=32 << 20),
        name="sweep",
    )(
        steps,
        pair_tile[0, 0],
        pair_turbine[0, 0],
        adjoint_init,
        saved_states,
        edge_halo,
        core_halo,
        near_halo,
        odd_halo,
        even_halo,
        whi,
        wlo,
        dz,
        disk_filter[0, 0],
    )
    part = jnp.sum(lax.all_to_all(part, NEAR_AXES, 0, 0, tiled=True), axis=0)
    part = jnp.broadcast_to(part[None], (wide, 128))
    totals = jnp.sum(lax.all_to_all(part, FAR_AXES, 0, 0, tiled=True), axis=0)[:turbines]
    turbine_grad = jnp.where(mine > 0.0, totals, jnp.float32(0.0))[None, None, :]
    return (adjoint, turbine_grad)


def solution(mesh):
    torus = Mesh(
        mesh.devices.reshape(4, 4, 2, 2, mesh.shape["gy"]), ("gx_0", "gx_1", "gx_2", "gx_3", "gy")
    )
    placed = (
        P(None, GX, "gy", None),
        P(None, None, GX, "gy", None),
        P(),
        P(),
        P(GX, "gy", None, None, None),
        P(GX, "gy", None),
        P(GX, "gy", None),
        P(),
    )
    return jax.shard_map(
        body,
        mesh=torus,
        in_specs=placed,
        out_specs=(P(None, GX, "gy", None), P(GX, "gy", None)),
        check_vma=False,
    )
```

```python
import jax
import jax.numpy as jnp
from jax import lax
from jax.experimental import pallas as pl
from jax.experimental.pallas import tpu as pltpu
from jax.sharding import Mesh
from jax.sharding import PartitionSpec as P

STEPS = 4
GX = ("gx_0", "gx_1", "gx_2", "gx_3")
NEAR_AXES = ("gx_0", "gx_1", "gx_3")
FAR_AXES = ("gx_2", "gy")
TENTH = 0.2 * 0.5
LEVELS = 256
RADII = (4, 4, 3, 2, 1, 1)
REST = 5


def padded(rows):
    return (rows + 15) // 16 * 16


def enumerate_runs(lengths):
    offsets, at = {}, 0
    for key, length in lengths:
        offsets[key] = at
        at += length
    return offsets, padded(at)


EDGE_RUNS, EDGE_ROWS = enumerate_runs(
    ((f, c, d, k), r - d) for f, r in enumerate(RADII) for c in range(3) for d in range(1, r) for k in range(2)
)
CORE_RUNS, CORE_ROWS = enumerate_runs(
    ((f, c, d), 8 - 2 * (r - d)) for f, r in enumerate(RADII) for c in range(3) for d in range(1, r + 1)
)
NEAR_RUNS, NEAR_ROWS = enumerate_runs(
    ((f, c, d), 8) for f, r in enumerate(RADII) for c in range(3) for d in range(1, r + 1)
)
Y_RUNS, Y_ROWS = enumerate_runs(
    [((f, c, d), 8) for f, r in enumerate(RADII) for c in range(3) for d in range(1, r + 1)]
    + [((f, c, d, k), r - d) for f, r in enumerate(RADII) for c in range(3) for d in range(1, r) for k in range(2)]
)


def first_core():
    return lax.axis_index("gx_3") == 0


def even_slab():
    return lax.rem(lax.axis_index("gy"), 2) == 0


def own_column(steps, adj_ref, st_ref, first, field, c, p):
    x = jnp.where(first, p, 7 - p)
    if field == 0:
        return adj_ref[c, x]
    if field == REST:
        tile = adj_ref[c, x]
        return tile - tile.astype(jnp.bfloat16).astype(jnp.float32)
    return st_ref[steps[field - 1], c, x].astype(jnp.float32)


def pack_x(steps_ref, adj_ref, st_ref, edge_ref, core_ref, near_ref, edge, core, steps, adj, st, sems):
    first = first_core()
    copies = (
        pltpu.make_async_copy(steps_ref, steps, sems.at[0]),
        pltpu.make_async_copy(adj_ref, adj, sems.at[1]),
        pltpu.make_async_copy(st_ref, st, sems.at[2]),
    )
    for copy in copies:
        copy.start()
    for copy in copies:
        copy.wait()
    for field, radius in enumerate(RADII):
        for c in range(3):
            for d in range(1, radius + 1):
                tile = own_column(steps, adj, st, first, field, c, d - 1)
                length = radius - d
                if length:
                    at = EDGE_RUNS[field, c, d, 0]
                    edge[at : at + length, :] = tile[:length]
                    at = EDGE_RUNS[field, c, d, 1]
                    edge[at : at + length, :] = tile[8 - length :]
                at = CORE_RUNS[field, c, d]
                core[at : at + 8 - 2 * length, :] = tile[length : 8 - length]
                at = NEAR_RUNS[field, c, d]
                near_ref[at : at + 8, :] = own_column(steps, adj, st, first, field, c, 8 - d).astype(jnp.bfloat16)
    edge_ref[...] = edge[...].astype(jnp.bfloat16)
    core_ref[...] = core[...].astype(jnp.bfloat16)


def pack_y(steps, adj_ref, st_ref, edge_ref, near_ref, odd_ref, even_ref, wide, edge, flat):
    first, even = first_core(), even_slab()
    edge[...] = edge_ref[...].astype(jnp.float32)

    def put(field, c, at, rows):
        wide[field, c, 0, at, :] = rows[:, :128]
        wide[field, c, 1, at, :] = rows[:, 128:]

    for field, radius in enumerate(RADII):
        for c in range(3):
            for p in range(8):
                at = (p + 4) * 8
                put(field, c, slice(at, at + 8), own_column(steps, adj_ref, st_ref, first, field, c, p))
            for d in range(1, radius):
                length = radius - d
                at = (4 - d) * 8
                run = EDGE_RUNS[field, c, d, 0]
                put(field, c, slice(at, at + length), edge[run : run + length, :])
                run = EDGE_RUNS[field, c, d, 1]
                put(field, c, slice(at + 8 - length, at + 8), edge[run : run + length, :])
                at, run = (11 + d) * 8, NEAR_RUNS[field, c, d]
                put(field, c, slice(at, at + 8), near_ref[run : run + 8, :].astype(jnp.float32))

    def take(field, c, run, start, length):
        at = pl.ds(start, length, stride=8)
        flat[run : run + length, 0:128] = wide[field, c, 0, at, :]
        flat[run : run + length, 128:256] = wide[field, c, 1, at, :]

    for side, out in enumerate((odd_ref, even_ref)):
        up = even if side else jnp.logical_not(even)
        for field, radius in enumerate(RADII):
            for c in range(3):
                for d in range(1, radius + 1):
                    y = jnp.where(up, 8 - d, d - 1)
                    length = radius - d
                    take(field, c, Y_RUNS[field, c, d], 4 * 8 + y, 8)
                    if length:
                        take(field, c, Y_RUNS[field, c, d, 0], (4 - length) * 8 + y, length)
                        take(field, c, Y_RUNS[field, c, d, 1], 12 * 8 + y, length)
        out[...] = flat[...].astype(jnp.bfloat16)


def prepare(inverse_ref, owner_ref, filt_ref, weights_ref, dz_ref, mine_ref, staged_ref):
    inverse = inverse_ref[...]
    k = lax.broadcasted_iota(jnp.int32, (LEVELS, LEVELS), 0)
    z = lax.broadcasted_iota(jnp.int32, (LEVELS, LEVELS), 1)
    above = jnp.where(z < LEVELS - 1, pltpu.roll(inverse, LEVELS - 1, 1), 0.0)
    below = jnp.where(z > 0, pltpu.roll(inverse, 1, 1), 0.0)
    for half, weights in enumerate((inverse, above - below)):
        lanes = slice(half * LEVELS, (half + 1) * LEVELS)
        upper = weights.astype(jnp.bfloat16)
        weights_ref[0:LEVELS, lanes] = upper
        weights_ref[LEVELS : 2 * LEVELS, lanes] = upper
        weights_ref[2 * LEVELS :, lanes] = (weights - upper.astype(jnp.float32)).astype(jnp.bfloat16)
    dz = (k == z + 1).astype(jnp.float32) - (k == z - 1).astype(jnp.float32)
    dz_ref[...] = dz.astype(jnp.bfloat16)
    own_index = lax.axis_index(GX) * lax.axis_size("gy") + lax.axis_index("gy")
    mine_ref[...] = (owner_ref[...] == own_index).astype(jnp.float32)
    staged_ref[...] = filt_ref[...]


def rest_reach(e):
    p = e - 4
    return max(0, RADII[REST] - max(0, -p, p - 7))


def sweep(
    steps,
    slots,
    adj_ref,
    st_ref,
    edge_ref,
    core_ref,
    near_ref,
    odd_ref,
    even_ref,
    weights_ref,
    dz_ref,
    filt_ref,
    out_ref,
    part_ref,
    ext,
    solved,
    state_dz,
    kept,
    picked,
    edge,
    core,
    flat,
    wide,
):
    first, even = first_core(), even_slab()
    sign = jnp.where(first, 1.0, -1.0).astype(jnp.float32)
    edge[...] = edge_ref[...].astype(jnp.float32)
    core[...] = core_ref[...].astype(jnp.float32)
    for field, radius in enumerate(RADII):
        into = 0 if field == REST else field

        def put(c, at, rows):
            old = ext[0, c, at, :] if field == REST else 0.0
            ext[into, c, at, :] = rows + old

        for c in range(3):
            if field != REST:
                for p in range(8):
                    put(c, slice((p + 4) * 16, (p + 4) * 16 + 8), own_column(steps, adj_ref, st_ref, first, field, c, p))
            for d in range(1, radius + 1):
                at, length = (4 - d) * 16, radius - d
                if length:
                    for k, y in ((0, 0), (1, 8 - length)):
                        run = EDGE_RUNS[field, c, d, k]
                        put(c, slice(at + y, at + y + length), edge[run : run + length, :])
                run = CORE_RUNS[field, c, d]
                put(c, slice(at + length, at + 8 - length), core[run : run + 8 - 2 * length, :])
                at, run = (11 + d) * 16, NEAR_RUNS[field, c, d]
                put(c, slice(at, at + 8), near_ref[run : run + 8, :].astype(jnp.float32))

    def spread(field, c, run, start, length):
        at = pl.ds(start, length, stride=8)
        wide[field, c, 0, at, :] = flat[run : run + length, 0:128]
        wide[field, c, 1, at, :] = flat[run : run + length, 128:256]

    for side, halo in enumerate((odd_ref, even_ref)):
        up = even if side else jnp.logical_not(even)
        flat[...] = halo[...].astype(jnp.float32)
        for field, radius in enumerate(RADII):
            for c in range(3):
                for d in range(1, radius + 1):
                    y = jnp.where(up, d - 1, 8 - d)
                    length = radius - d
                    spread(field, c, Y_RUNS[field, c, d], 4 * 8 + y, 8)
                    if length:
                        spread(field, c, Y_RUNS[field, c, d, 0], (4 - length) * 8 + y, length)
                        spread(field, c, Y_RUNS[field, c, d, 1], 12 * 8 + y, length)
    for field, radius in enumerate(RADII[:REST]):
        for c in range(3):
            for e in range(5 - radius, 11 + radius):
                for half in range(2):
                    rows = wide[field, c, half, e * 8 : e * 8 + 8, :]
                    if field == 0:
                        near_rows = wide[REST, c, half, e * 8 : e * 8 + 8, :]
                        y = lax.broadcasted_iota(jnp.int32, (8, 128), 0)
                        reach = rest_reach(e)
                        if reach:
                            rows += jnp.where((y < reach) | (y >= 8 - reach), near_rows, 0.0)
                    ext[field, c, e * 16 + 8 : e * 16 + 16, half * 128 : half * 128 + 128] = rows

    for step in range(STEPS):
        reach = 3 - step
        lo, hi = 4 - reach, 12 + reach
        span = hi - lo + 2
        rows = ext[0, :, (lo - 1) * 16 : (hi + 1) * 16, :].reshape(3 * span * 16, LEVELS)
        upper = rows.astype(jnp.bfloat16)
        lower = (rows - upper.astype(jnp.float32)).astype(jnp.bfloat16)
        stacked = jnp.concatenate([upper, lower, upper], axis=1)
        for half in range(2):
            lanes = slice(half * LEVELS, (half + 1) * LEVELS)
            total = jnp.dot(stacked, weights_ref[:, lanes], preferred_element_type=jnp.float32)
            solved[half, :, (lo - 1) * 16 : (hi + 1) * 16, :] = total.reshape(3, span * 16, LEVELS)
        field = 1 + step
        states = ext[field, :, lo * 16 : hi * 16, :].reshape(3 * (span - 2) * 16, LEVELS).astype(jnp.bfloat16)
        state_dz[:, lo * 16 : hi * 16, :] = jnp.dot(
            states, dz_ref[...], preferred_element_type=jnp.float32
        ).reshape(3, (span - 2) * 16, LEVELS)

        def one(e, carry):
            def at(ref, *lead, shift=0):
                return ref[(*lead, pl.ds(pl.multiple_of((e + shift) * 16, 16), 16), slice(None))]

            def across(ref, *lead):
                return at(ref, *lead, shift=1) - at(ref, *lead, shift=-1)

            def along(tile):
                return pltpu.roll(tile, 15, 0) - pltpu.roll(tile, 1, 0)

            sol = [at(solved, 0, c) for c in range(3)]
            vel = [at(ext, field, c) for c in range(3)]
            derivs = (
                [across(ext, field, c) for c in range(3)],
                [along(vel[c]) for c in range(3)],
                [at(state_dz, c) for c in range(3)],
            )
            stream = sign * vel[0]
            for c in range(3):
                advect = stream * across(solved, 0, c) + vel[1] * along(sol[c]) + vel[2] * at(solved, 1, c)
                couple = sol[0] * derivs[c][0] + sol[1] * derivs[c][1] + sol[2] * derivs[c][2]
                if c == 0:
                    couple = sign * couple
                ext[0, c, pl.ds(pl.multiple_of(e * 16, 16), 16), :] = sol[c] + TENTH * (advect - couple)
            return carry

        lax.fori_loop(lo, hi, one, 0, unroll=2)
        for p in range(8):
            kept[step, p * 8 : p * 8 + 8, :] = ext[0, 0, (p + 4) * 16 : (p + 4) * 16 + 8, :]

    for c in range(3):
        for p in range(8):
            out_ref[c, jnp.where(first, p, 7 - p)] = ext[0, c, (p + 4) * 16 : (p + 4) * 16 + 8, :]
    lane = lax.broadcasted_iota(jnp.int32, (1, 128), 1)
    total = jnp.zeros((1, 128), jnp.float32)
    for slot in range(8):
        tile = slots[slot]
        x, y = tile // 4, 2 * lax.rem(tile, 4)
        p = jnp.where(first, x, 7 - x)
        for step in range(STEPS):
            for k in range(2):
                lanes = slice(k * LEVELS, (k + 1) * LEVELS)
                picked[slot, step : step + 1, lanes] = kept[step, pl.ds(p * 8 + y + k, 1), :]
                picked[slot, 4 + step : 5 + step, lanes] = ext[1 + step, 0, pl.ds((p + 4) * 16 + y + k, 1), :]
        both = lax.dot_general(
            picked[slot].astype(jnp.bfloat16),
            filt_ref[slot],
            (((1,), (1,)), ((), ())),
            preferred_element_type=jnp.float32,
        )
        sampled, speeds = both[0:4], both[4:8]
        term = jnp.sum(jnp.sum(speeds * speeds * sampled, axis=1, keepdims=True), axis=0, keepdims=True)
        total += jnp.where(lane == slots[8 + slot], term * (1.0 / 64.0), 0.0)
    part_ref[...] = jnp.broadcast_to(total, part_ref.shape)


SMEM = pl.BlockSpec(memory_space=pltpu.SMEM)
VMEM = pl.BlockSpec(memory_space=pltpu.VMEM)


def halo_rows(rows):
    return jax.ShapeDtypeStruct((rows, LEVELS), jnp.bfloat16)


def body(
    adjoint_init,
    saved_states,
    step_index,
    vertical_inverse,
    disk_filter,
    pair_turbine,
    pair_tile,
    turbine_owner,
):
    turbines = turbine_owner.shape[0]
    steps = step_index.astype(jnp.int32)
    blocks, slabs = lax.axis_size(GX), lax.axis_size("gy")
    near = [(i, i ^ 1) for i in range(blocks)]
    far = [(i, (i + 1) % blocks if i % 2 else (i - 1) % blocks) for i in range(blocks)]
    evens = [(i, i ^ 1) for i in range(slabs)]
    odds = [(i, (i + 1) % slabs if i % 2 else (i - 1) % slabs) for i in range(slabs)]

    to_edge, to_core, to_near = pl.pallas_call(
        pack_x,
        out_shape=(halo_rows(EDGE_ROWS), halo_rows(CORE_ROWS), halo_rows(NEAR_ROWS)),
        in_specs=[pl.BlockSpec(memory_space=pl.ANY)] * 3,
        out_specs=(VMEM,) * 3,
        scratch_shapes=[
            pltpu.VMEM((EDGE_ROWS, LEVELS), jnp.float32),
            pltpu.VMEM((CORE_ROWS, LEVELS), jnp.float32),
            pltpu.SMEM((STEPS,), jnp.int32),
            pltpu.VMEM(adjoint_init.shape, jnp.float32),
            pltpu.VMEM(saved_states.shape, jnp.bfloat16),
            pltpu.SemaphoreType.DMA((3,)),
        ],
        compiler_params=pltpu.CompilerParams(vmem_limit_bytes=67043328),
        name="pack_x",
    )(steps, adjoint_init, saved_states)
    edge_halo = lax.ppermute(to_edge, GX, far)
    near_halo = lax.ppermute(to_near, GX, near)
    core_halo = lax.ppermute(to_core, GX, far)

    filters = disk_filter[0, 0]
    weights, dz, mine, filters = pl.pallas_call(
        prepare,
        out_shape=(
            jax.ShapeDtypeStruct((3 * LEVELS, 2 * LEVELS), jnp.bfloat16),
            jax.ShapeDtypeStruct((LEVELS, LEVELS), jnp.bfloat16),
            jax.ShapeDtypeStruct((1, turbines), jnp.float32),
            jax.ShapeDtypeStruct(filters.shape, jnp.bfloat16),
        ),
        in_specs=[VMEM] * 3,
        out_specs=(VMEM,) * 4,
        compiler_params=pltpu.CompilerParams(vmem_limit_bytes=4 << 20),
        name="prepare",
    )(vertical_inverse, turbine_owner[None], filters)

    to_odd, to_even = pl.pallas_call(
        pack_y,
        out_shape=(halo_rows(Y_ROWS), halo_rows(Y_ROWS)),
        in_specs=[SMEM] + [VMEM] * 4,
        out_specs=(VMEM, VMEM),
        scratch_shapes=[
            pltpu.VMEM((len(RADII), 3, 2, 128, 128), jnp.float32),
            pltpu.VMEM((EDGE_ROWS, LEVELS), jnp.float32),
            pltpu.VMEM((Y_ROWS, LEVELS), jnp.float32),
        ],
        compiler_params=pltpu.CompilerParams(vmem_limit_bytes=16 << 20),
        name="pack_y",
    )(steps, adjoint_init, saved_states, edge_halo, near_halo)
    odd_halo = lax.ppermute(to_odd, "gy", odds)
    even_halo = lax.ppermute(to_even, "gy", evens)

    slots = jnp.concatenate([pair_tile[0, 0], pair_turbine[0, 0]])
    odd_halo, slots = lax.optimization_barrier((odd_halo, slots))
    close = lax.axis_size(NEAR_AXES)
    wide = lax.axis_size(FAR_AXES)
    adjoint, part = pl.pallas_call(
        sweep,
        out_shape=(
            jax.ShapeDtypeStruct(adjoint_init.shape, jnp.float32),
            jax.ShapeDtypeStruct((close, 128), jnp.float32),
        ),
        in_specs=[SMEM] * 2 + [VMEM] * 10,
        out_specs=(VMEM, VMEM),
        scratch_shapes=[
            pltpu.VMEM((5, 3, 256, LEVELS), jnp.float32),
            pltpu.VMEM((2, 3, 256, LEVELS), jnp.float32),
            pltpu.VMEM((3, 256, LEVELS), jnp.float32),
            pltpu.VMEM((STEPS, 64, LEVELS), jnp.float32),
            pltpu.VMEM((8, 8, 2 * LEVELS), jnp.float32),
            pltpu.VMEM((EDGE_ROWS, LEVELS), jnp.float32),
            pltpu.VMEM((CORE_ROWS, LEVELS), jnp.float32),
            pltpu.VMEM((Y_ROWS, LEVELS), jnp.float32),
            pltpu.VMEM((len(RADII), 3, 2, 128, 128), jnp.float32),
        ],
        compiler_params=pltpu.CompilerParams(vmem_limit_bytes=32 << 20),
        name="sweep",
    )(
        steps,
        slots,
        adjoint_init,
        saved_states,
        edge_halo,
        core_halo,
        near_halo,
        odd_halo,
        even_halo,
        weights,
        dz,
        filters,
    )
    part = jnp.sum(lax.all_to_all(part, NEAR_AXES, 0, 0, tiled=True), axis=0)
    part = jnp.broadcast_to(part[None], (wide, 128))
    totals = jnp.sum(lax.all_to_all(part, FAR_AXES, 0, 0, tiled=True), axis=0)[:turbines]
    turbine_grad = jnp.where(mine[0] > 0.0, totals, jnp.float32(0.0))[None, None, :]
    return (adjoint, turbine_grad)


def solution(mesh):
    torus = Mesh(
        mesh.devices.reshape(4, 4, 2, 2, mesh.shape["gy"]), ("gx_0", "gx_1", "gx_2", "gx_3", "gy")
    )
    placed = (
        P(None, GX, "gy", None),
        P(None, None, GX, "gy", None),
        P(),
        P(),
        P(GX, "gy", None, None, None),
        P(GX, "gy", None),
        P(GX, "gy", None),
        P(),
    )
    return jax.shard_map(
        body,
        mesh=torus,
        in_specs=placed,
        out_specs=(P(None, GX, "gy", None), P(GX, "gy", None)),
        check_vma=False,
    )
```

```python
import jax
import jax.numpy as jnp
from jax import lax
from jax.experimental import pallas as pl
from jax.experimental.pallas import tpu as pltpu
from jax.sharding import Mesh
from jax.sharding import PartitionSpec as P

STEPS = 4
GX = ("gx_0", "gx_1", "gx_2", "gx_3")
NEAR_AXES = ("gx_0", "gx_1", "gx_3")
FAR_AXES = ("gx_2", "gy")
TENTH = 0.2 * 0.5
LEVELS = 256
RADII = (4, 4, 3, 2, 1, 1)
REST = 5


def padded(rows):
    return (rows + 15) // 16 * 16


def enumerate_runs(lengths):
    offsets, at = {}, 0
    for key, length in lengths:
        offsets[key] = at
        at += length
    return offsets, padded(at)


EDGE_RUNS, EDGE_ROWS = enumerate_runs(
    ((f, c, d, k), r - d) for f, r in enumerate(RADII) for c in range(3) for d in range(1, r) for k in range(2)
)
CORE_RUNS, CORE_ROWS = enumerate_runs(
    ((f, c, d), 8 - 2 * (r - d)) for f, r in enumerate(RADII) for c in range(3) for d in range(1, r + 1)
)
NEAR_RUNS, NEAR_ROWS = enumerate_runs(
    ((f, c, d), 8) for f, r in enumerate(RADII) for c in range(3) for d in range(1, r + 1)
)
Y_RUNS, Y_ROWS = enumerate_runs(
    [((f, c, d), 8) for f, r in enumerate(RADII) for c in range(3) for d in range(1, r + 1)]
    + [((f, c, d, k), r - d) for f, r in enumerate(RADII) for c in range(3) for d in range(1, r) for k in range(2)]
)


def first_core():
    return lax.axis_index("gx_3") == 0


def even_slab():
    return lax.rem(lax.axis_index("gy"), 2) == 0


def own_column(steps, adj_ref, st_ref, first, field, c, p):
    x = jnp.where(first, p, 7 - p)
    if field == 0:
        return adj_ref[c, x]
    if field == REST:
        tile = adj_ref[c, x]
        return tile - tile.astype(jnp.bfloat16).astype(jnp.float32)
    return st_ref[steps[field - 1], c, x].astype(jnp.float32)


def pack_x(steps_ref, adj_ref, st_ref, edge_ref, core_ref, near_ref, edge, core, steps, adj, st, sems):
    first = first_core()
    copies = (
        pltpu.make_async_copy(steps_ref, steps, sems.at[0]),
        pltpu.make_async_copy(adj_ref, adj, sems.at[1]),
        pltpu.make_async_copy(st_ref, st, sems.at[2]),
    )
    for copy in copies:
        copy.start()
    for copy in copies:
        copy.wait()
    for field, radius in enumerate(RADII):
        for c in range(3):
            for d in range(1, radius + 1):
                tile = own_column(steps, adj, st, first, field, c, d - 1)
                length = radius - d
                if length:
                    at = EDGE_RUNS[field, c, d, 0]
                    edge[at : at + length, :] = tile[:length]
                    at = EDGE_RUNS[field, c, d, 1]
                    edge[at : at + length, :] = tile[8 - length :]
                at = CORE_RUNS[field, c, d]
                core[at : at + 8 - 2 * length, :] = tile[length : 8 - length]
                at = NEAR_RUNS[field, c, d]
                near_ref[at : at + 8, :] = own_column(steps, adj, st, first, field, c, 8 - d).astype(jnp.bfloat16)
    edge_ref[...] = edge[...].astype(jnp.bfloat16)
    core_ref[...] = core[...].astype(jnp.bfloat16)


def pack_y(steps, adj_ref, st_ref, edge_ref, near_ref, odd_ref, even_ref, wide, edge, flat):
    first, even = first_core(), even_slab()
    edge[...] = edge_ref[...].astype(jnp.float32)

    def put(field, c, at, rows):
        wide[field, c, 0, at, :] = rows[:, :128]
        wide[field, c, 1, at, :] = rows[:, 128:]

    for field, radius in enumerate(RADII):
        for c in range(3):
            for p in range(8):
                at = (p + 4) * 8
                put(field, c, slice(at, at + 8), own_column(steps, adj_ref, st_ref, first, field, c, p))
            for d in range(1, radius):
                length = radius - d
                at = (4 - d) * 8
                run = EDGE_RUNS[field, c, d, 0]
                put(field, c, slice(at, at + length), edge[run : run + length, :])
                run = EDGE_RUNS[field, c, d, 1]
                put(field, c, slice(at + 8 - length, at + 8), edge[run : run + length, :])
                at, run = (11 + d) * 8, NEAR_RUNS[field, c, d]
                put(field, c, slice(at, at + 8), near_ref[run : run + 8, :].astype(jnp.float32))

    def take(field, c, run, start, length):
        at = pl.ds(start, length, stride=8)
        flat[run : run + length, 0:128] = wide[field, c, 0, at, :]
        flat[run : run + length, 128:256] = wide[field, c, 1, at, :]

    for side, out in enumerate((odd_ref, even_ref)):
        up = even if side else jnp.logical_not(even)
        for field, radius in enumerate(RADII):
            for c in range(3):
                for d in range(1, radius + 1):
                    y = jnp.where(up, 8 - d, d - 1)
                    length = radius - d
                    take(field, c, Y_RUNS[field, c, d], 4 * 8 + y, 8)
                    if length:
                        take(field, c, Y_RUNS[field, c, d, 0], (4 - length) * 8 + y, length)
                        take(field, c, Y_RUNS[field, c, d, 1], 12 * 8 + y, length)
        out[...] = flat[...].astype(jnp.bfloat16)


def prepare(inverse_ref, owner_ref, filt_ref, weights_ref, dz_ref, mine_ref, staged_ref):
    inverse = inverse_ref[...]
    k = lax.broadcasted_iota(jnp.int32, (LEVELS, LEVELS), 0)
    z = lax.broadcasted_iota(jnp.int32, (LEVELS, LEVELS), 1)
    above = jnp.where(z < LEVELS - 1, pltpu.roll(inverse, LEVELS - 1, 1), 0.0)
    below = jnp.where(z > 0, pltpu.roll(inverse, 1, 1), 0.0)
    for half, weights in enumerate((inverse, above - below)):
        lanes = slice(half * LEVELS, (half + 1) * LEVELS)
        upper = weights.astype(jnp.bfloat16)
        weights_ref[0:LEVELS, lanes] = upper
        weights_ref[LEVELS : 2 * LEVELS, lanes] = upper
        weights_ref[2 * LEVELS :, lanes] = (weights - upper.astype(jnp.float32)).astype(jnp.bfloat16)
    dz = (k == z + 1).astype(jnp.float32) - (k == z - 1).astype(jnp.float32)
    dz_ref[...] = dz.astype(jnp.bfloat16)
    own_index = lax.axis_index(GX) * lax.axis_size("gy") + lax.axis_index("gy")
    mine_ref[...] = (owner_ref[...] == own_index).astype(jnp.float32)
    staged_ref[...] = filt_ref[...]


def rest_reach(e):
    p = e - 4
    return max(0, RADII[REST] - max(0, -p, p - 7))


def sweep(
    steps,
    slots,
    adj_ref,
    st_ref,
    edge_ref,
    core_ref,
    near_ref,
    odd_ref,
    even_ref,
    weights_ref,
    dz_ref,
    filt_ref,
    out_ref,
    part_ref,
    ext,
    solved,
    state_dz,
    kept,
    picked,
    edge,
    core,
    flat,
    wide,
):
    first, even = first_core(), even_slab()
    sign = jnp.where(first, 1.0, -1.0).astype(jnp.float32)
    edge[...] = edge_ref[...].astype(jnp.float32)
    core[...] = core_ref[...].astype(jnp.float32)
    for field, radius in enumerate(RADII):
        into = 0 if field == REST else field

        def put(c, at, rows):
            old = ext[0, c, at, :] if field == REST else 0.0
            ext[into, c, at, :] = rows + old

        for c in range(3):
            if field != REST:
                for p in range(8):
                    put(c, slice((p + 4) * 16, (p + 4) * 16 + 8), own_column(steps, adj_ref, st_ref, first, field, c, p))
            for d in range(1, radius + 1):
                at, length = (4 - d) * 16, radius - d
                if length:
                    for k, y in ((0, 0), (1, 8 - length)):
                        run = EDGE_RUNS[field, c, d, k]
                        put(c, slice(at + y, at + y + length), edge[run : run + length, :])
                run = CORE_RUNS[field, c, d]
                put(c, slice(at + length, at + 8 - length), core[run : run + 8 - 2 * length, :])
                at, run = (11 + d) * 16, NEAR_RUNS[field, c, d]
                put(c, slice(at, at + 8), near_ref[run : run + 8, :].astype(jnp.float32))

    def spread(field, c, run, start, length):
        at = pl.ds(start, length, stride=8)
        wide[field, c, 0, at, :] = flat[run : run + length, 0:128]
        wide[field, c, 1, at, :] = flat[run : run + length, 128:256]

    for side, halo in enumerate((odd_ref, even_ref)):
        up = even if side else jnp.logical_not(even)
        flat[...] = halo[...].astype(jnp.float32)
        for field, radius in enumerate(RADII):
            for c in range(3):
                for d in range(1, radius + 1):
                    y = jnp.where(up, d - 1, 8 - d)
                    length = radius - d
                    spread(field, c, Y_RUNS[field, c, d], 4 * 8 + y, 8)
                    if length:
                        spread(field, c, Y_RUNS[field, c, d, 0], (4 - length) * 8 + y, length)
                        spread(field, c, Y_RUNS[field, c, d, 1], 12 * 8 + y, length)
    for field, radius in enumerate(RADII[:REST]):
        for c in range(3):
            for e in range(5 - radius, 11 + radius):
                for half in range(2):
                    rows = wide[field, c, half, e * 8 : e * 8 + 8, :]
                    if field == 0:
                        near_rows = wide[REST, c, half, e * 8 : e * 8 + 8, :]
                        y = lax.broadcasted_iota(jnp.int32, (8, 128), 0)
                        reach = rest_reach(e)
                        if reach:
                            rows += jnp.where((y < reach) | (y >= 8 - reach), near_rows, 0.0)
                    ext[field, c, e * 16 + 8 : e * 16 + 16, half * 128 : half * 128 + 128] = rows

    for step in range(STEPS):
        reach = 3 - step
        lo, hi = 4 - reach, 12 + reach
        span = hi - lo + 2
        rows = ext[0, :, (lo - 1) * 16 : (hi + 1) * 16, :].reshape(3 * span * 16, LEVELS)
        upper = rows.astype(jnp.bfloat16)
        lower = (rows - upper.astype(jnp.float32)).astype(jnp.bfloat16)
        stacked = jnp.concatenate([upper, lower, upper], axis=1)
        for half in range(2):
            lanes = slice(half * LEVELS, (half + 1) * LEVELS)
            total = jnp.dot(stacked, weights_ref[:, lanes], preferred_element_type=jnp.float32)
            solved[half, :, (lo - 1) * 16 : (hi + 1) * 16, :] = total.reshape(3, span * 16, LEVELS)
        field = 1 + step
        states = ext[field, :, lo * 16 : hi * 16, :].reshape(3 * (span - 2) * 16, LEVELS).astype(jnp.bfloat16)
        state_dz[:, lo * 16 : hi * 16, :] = jnp.dot(
            states, dz_ref[...], preferred_element_type=jnp.float32
        ).reshape(3, (span - 2) * 16, LEVELS)

        def one(e, carry):
            def at(ref, *lead, shift=0):
                return ref[(*lead, pl.ds(pl.multiple_of((e + shift) * 16, 16), 16), slice(None))]

            def across(ref, *lead):
                return at(ref, *lead, shift=1) - at(ref, *lead, shift=-1)

            def along(tile):
                return pltpu.roll(tile, 15, 0) - pltpu.roll(tile, 1, 0)

            sol = [at(solved, 0, c) for c in range(3)]
            vel = [at(ext, field, c) for c in range(3)]
            derivs = (
                [across(ext, field, c) for c in range(3)],
                [along(vel[c]) for c in range(3)],
                [at(state_dz, c) for c in range(3)],
            )
            keep = 8 if step == STEPS - 1 else 16
            stream = sign * vel[0]
            for c in range(3):
                advect = stream * across(solved, 0, c) + vel[1] * along(sol[c]) + vel[2] * at(solved, 1, c)
                couple = sol[0] * derivs[c][0] + sol[1] * derivs[c][1] + sol[2] * derivs[c][2]
                if c == 0:
                    couple = sign * couple
                ext[0, c, pl.ds(pl.multiple_of(e * 16, 16), keep), :] = (
                    sol[c][:keep] + TENTH * (advect[:keep] - couple[:keep])
                )
            return carry

        lax.fori_loop(lo, hi, one, 0, unroll=(2, 4, 2, 4)[step])
        for p in range(8):
            kept[step, p * 8 : p * 8 + 8, :] = ext[0, 0, (p + 4) * 16 : (p + 4) * 16 + 8, :]

    for c in range(3):
        for p in range(8):
            out_ref[c, jnp.where(first, p, 7 - p)] = ext[0, c, (p + 4) * 16 : (p + 4) * 16 + 8, :]
    lane = lax.broadcasted_iota(jnp.int32, (1, 128), 1)
    total = jnp.zeros((1, 128), jnp.float32)
    for slot in range(8):
        tile = slots[slot]
        x, y = tile // 4, 2 * lax.rem(tile, 4)
        p = jnp.where(first, x, 7 - x)
        for step in range(STEPS):
            for k in range(2):
                lanes = slice(k * LEVELS, (k + 1) * LEVELS)
                picked[slot, step : step + 1, lanes] = kept[step, pl.ds(p * 8 + y + k, 1), :]
                picked[slot, 4 + step : 5 + step, lanes] = ext[1 + step, 0, pl.ds((p + 4) * 16 + y + k, 1), :]
        both = lax.dot_general(
            picked[slot].astype(jnp.bfloat16),
            filt_ref[slot],
            (((1,), (1,)), ((), ())),
            preferred_element_type=jnp.float32,
        )
        sampled, speeds = both[0:4], both[4:8]
        term = jnp.sum(jnp.sum(speeds * speeds * sampled, axis=1, keepdims=True), axis=0, keepdims=True)
        total += jnp.where(lane == slots[8 + slot], term * (1.0 / 64.0), 0.0)
    part_ref[...] = jnp.broadcast_to(total, part_ref.shape)


SMEM = pl.BlockSpec(memory_space=pltpu.SMEM)
VMEM = pl.BlockSpec(memory_space=pltpu.VMEM)


def halo_rows(rows):
    return jax.ShapeDtypeStruct((rows, LEVELS), jnp.bfloat16)


def body(
    adjoint_init,
    saved_states,
    step_index,
    vertical_inverse,
    disk_filter,
    pair_turbine,
    pair_tile,
    turbine_owner,
):
    turbines = turbine_owner.shape[0]
    steps = step_index.astype(jnp.int32)
    blocks, slabs = lax.axis_size(GX), lax.axis_size("gy")
    near = [(i, i ^ 1) for i in range(blocks)]
    far = [(i, (i + 1) % blocks if i % 2 else (i - 1) % blocks) for i in range(blocks)]
    evens = [(i, i ^ 1) for i in range(slabs)]
    odds = [(i, (i + 1) % slabs if i % 2 else (i - 1) % slabs) for i in range(slabs)]

    to_edge, to_core, to_near = pl.pallas_call(
        pack_x,
        out_shape=(halo_rows(EDGE_ROWS), halo_rows(CORE_ROWS), halo_rows(NEAR_ROWS)),
        in_specs=[pl.BlockSpec(memory_space=pl.ANY)] * 3,
        out_specs=(VMEM,) * 3,
        scratch_shapes=[
            pltpu.VMEM((EDGE_ROWS, LEVELS), jnp.float32),
            pltpu.VMEM((CORE_ROWS, LEVELS), jnp.float32),
            pltpu.SMEM((STEPS,), jnp.int32),
            pltpu.VMEM(adjoint_init.shape, jnp.float32),
            pltpu.VMEM(saved_states.shape, jnp.bfloat16),
            pltpu.SemaphoreType.DMA((3,)),
        ],
        compiler_params=pltpu.CompilerParams(vmem_limit_bytes=67043328),
        name="pack_x",
    )(steps, adjoint_init, saved_states)
    edge_halo = lax.ppermute(to_edge, GX, far)
    near_halo = lax.ppermute(to_near, GX, near)
    core_halo = lax.ppermute(to_core, GX, far)

    filters = disk_filter[0, 0]
    weights, dz, mine, filters = pl.pallas_call(
        prepare,
        out_shape=(
            jax.ShapeDtypeStruct((3 * LEVELS, 2 * LEVELS), jnp.bfloat16),
            jax.ShapeDtypeStruct((LEVELS, LEVELS), jnp.bfloat16),
            jax.ShapeDtypeStruct((1, turbines), jnp.float32),
            jax.ShapeDtypeStruct(filters.shape, jnp.bfloat16),
        ),
        in_specs=[VMEM] * 3,
        out_specs=(VMEM,) * 4,
        compiler_params=pltpu.CompilerParams(vmem_limit_bytes=4 << 20),
        name="prepare",
    )(vertical_inverse, turbine_owner[None], filters)

    to_odd, to_even = pl.pallas_call(
        pack_y,
        out_shape=(halo_rows(Y_ROWS), halo_rows(Y_ROWS)),
        in_specs=[SMEM] + [VMEM] * 4,
        out_specs=(VMEM, VMEM),
        scratch_shapes=[
            pltpu.VMEM((len(RADII), 3, 2, 128, 128), jnp.float32),
            pltpu.VMEM((EDGE_ROWS, LEVELS), jnp.float32),
            pltpu.VMEM((Y_ROWS, LEVELS), jnp.float32),
        ],
        compiler_params=pltpu.CompilerParams(vmem_limit_bytes=16 << 20),
        name="pack_y",
    )(steps, adjoint_init, saved_states, edge_halo, near_halo)
    odd_halo = lax.ppermute(to_odd, "gy", odds)
    even_halo = lax.ppermute(to_even, "gy", evens)

    slots = jnp.concatenate([pair_tile[0, 0], pair_turbine[0, 0]])
    odd_halo, slots = lax.optimization_barrier((odd_halo, slots))
    close = lax.axis_size(NEAR_AXES)
    wide = lax.axis_size(FAR_AXES)
    adjoint, part = pl.pallas_call(
        sweep,
        out_shape=(
            jax.ShapeDtypeStruct(adjoint_init.shape, jnp.float32),
            jax.ShapeDtypeStruct((close, 128), jnp.float32),
        ),
        in_specs=[SMEM] * 2 + [VMEM] * 10,
        out_specs=(VMEM, VMEM),
        scratch_shapes=[
            pltpu.VMEM((5, 3, 256, LEVELS), jnp.float32),
            pltpu.VMEM((2, 3, 256, LEVELS), jnp.float32),
            pltpu.VMEM((3, 256, LEVELS), jnp.float32),
            pltpu.VMEM((STEPS, 64, LEVELS), jnp.float32),
            pltpu.VMEM((8, 8, 2 * LEVELS), jnp.float32),
            pltpu.VMEM((EDGE_ROWS, LEVELS), jnp.float32),
            pltpu.VMEM((CORE_ROWS, LEVELS), jnp.float32),
            pltpu.VMEM((Y_ROWS, LEVELS), jnp.float32),
            pltpu.VMEM((len(RADII), 3, 2, 128, 128), jnp.float32),
        ],
        compiler_params=pltpu.CompilerParams(vmem_limit_bytes=32 << 20),
        name="sweep",
    )(
        steps,
        slots,
        adjoint_init,
        saved_states,
        edge_halo,
        core_halo,
        near_halo,
        odd_halo,
        even_halo,
        weights,
        dz,
        filters,
    )
    part = jnp.sum(lax.all_to_all(part, NEAR_AXES, 0, 0, tiled=True), axis=0)
    part = jnp.broadcast_to(part[None], (wide, 128))
    totals = jnp.sum(lax.all_to_all(part, FAR_AXES, 0, 0, tiled=True), axis=0)[:turbines]
    turbine_grad = jnp.where(mine[0] > 0.0, totals, jnp.float32(0.0))[None, None, :]
    return (adjoint, turbine_grad)


def solution(mesh):
    torus = Mesh(
        mesh.devices.reshape(4, 4, 2, 2, mesh.shape["gy"]), ("gx_0", "gx_1", "gx_2", "gx_3", "gy")
    )
    placed = (
        P(None, GX, "gy", None),
        P(None, None, GX, "gy", None),
        P(),
        P(),
        P(GX, "gy", None, None, None),
        P(GX, "gy", None),
        P(GX, "gy", None),
        P(),
    )
    return jax.shard_map(
        body,
        mesh=torus,
        in_specs=placed,
        out_specs=(P(None, GX, "gy", None), P(GX, "gy", None)),
        check_vma=False,
    )
```
